32 devices in a mesh: op: 8 (over z, y), right: 4 (over x, core).
Axes of the slice: x: 2, y: 2, z: 4, core: 2. Of those that a mesh axis runs over, the one named last changes fastest.
Arguments:
- psi: float32 [768, 4096], P('op', 'right'), may hold values from -6 to 6
- left_env: float32 [16, 768, 768], P('op', 'right'), may hold values from -0.109375 to 0.109375
- right_env: float32 [16, 4096, 1024], P('op', 'right'), may hold values from -0.1875 to 0.1875
- sector_lengths: int32 [4], replicated, may hold values from 128 to 384, as said below
- op_map: int32 [16, 4], replicated, may hold values from 0 to 3
Outputs:
- h_psi: float32 [768, 4096], P('op', 'right')
The draws below stay inside these ranges and needn't reach their ends.
Inputs may be any that keep to these rules, and one draw needn't show every extreme that they name: `sector_lengths`: one sector, at a position that varies between draws, holds 384 states; every other sector holds 128.
All inputs are finite; a program needn't handle non-finite values.
Results may differ from the reference program's by a relative error of at most 0.0003.
Values sent between devices are 32-bit elements; how exact they have to be, the bound alone decides.
No kernel may reach another device: no remote copies, remote signals or barrier semaphores. Data moves between devices by JAX's collectives and lax.ppermute only.
A program may use at most 64 MiB of HBM per device.

```python
import jax
import jax.numpy as jnp
from jax import lax

A = 768
B_DEV = 1024
SECTORS = 4
PANEL = 128
W = 16
B = 4096
N_RIGHT = 4


def draw_sector_lengths(key, part):
    chosen = jax.random.randint(jax.random.fold_in(key, 7), (), 0, SECTORS).astype(jnp.int32)
    places = jnp.arange(SECTORS, dtype=jnp.int32)
    largest = A - (SECTORS - 1) * PANEL
    return jnp.where(places == chosen, largest, PANEL).astype(jnp.int32)


def plant(entries, own_key, low, top_value):
    longest = entries.shape.index(max(entries.shape))
    spots = []
    for shift in (0, 1):
        where = [jax.random.randint(jax.random.fold_in(own_key, axis), (), 0, length) for axis, length in enumerate(entries.shape)]
        where[longest] = (where[longest] + shift) % entries.shape[longest]
        spots.append(tuple(where))
    return entries.at[spots[0]].set(low).at[spots[1]].set(top_value)


def level_of(rng, extent, shards, smallest, high):
    def one(position, blocks):
        draws = jax.random.uniform(jax.random.fold_in(jax.random.fold_in(rng, 6), position), (blocks,), jnp.float32, smallest / len(shards), high / len(shards))
        return jnp.repeat(jnp.exp(draws), extent[position] // blocks).reshape((-1,) + (1,) * (len(extent) - position - 1))

    level = one(*shards[0])
    for cut in shards[1:]:
        level = level * one(*cut)
    return level


def bell_draw(stream_key, shape, width, bound, cuts=(), kind=jnp.bfloat16):
    entries = width * jax.random.normal(stream_key, shape, jnp.float32)
    if cuts:
        entries = entries * level_of(stream_key, shape, cuts, -0.22, 0.18)
    return jnp.clip(entries, -bound, bound).astype(kind)


def setup_inputs(seed: int = 0) -> dict:
    seeds = jax.random.split(jax.random.key(seed), 6)
    psi = bell_draw(seeds[0], (A, B), 1.0, 6.0, ((0, 8), (1, 4)), jnp.float32)
    left_env = bell_draw(seeds[1], (W, A, A), (A * W // SECTORS) ** -0.5, 0.109375, ((0, 8), (1, 4)), jnp.float32)
    right_env = bell_draw(seeds[2], (W, B, B_DEV), B_DEV ** -0.5, 0.1875, ((0, 8), (1, 4)), jnp.float32)
    sector_lengths = draw_sector_lengths(jax.random.fold_in(seeds[5], 71), 0)
    op_map = plant(jax.random.randint(seeds[4], (W, SECTORS), 0, SECTORS), jax.random.fold_in(seeds[4], 1), 0, SECTORS - 1).astype(jnp.int32)
    return dict(psi=psi, left_env=left_env, right_env=right_env, sector_lengths=sector_lengths, op_map=op_map)


def sector_of(sector_lengths):
    ends = jnp.cumsum(sector_lengths).astype(jnp.int32)
    places = jnp.arange(A, dtype=jnp.int32)
    return jnp.sum((places[:, None] >= ends[None, :]).astype(jnp.int32), axis=1).astype(jnp.int32)


def reference(psi, left_env, right_env, sector_lengths, op_map):
    sector = sector_of(sector_lengths)
    blocks = psi.reshape(A, N_RIGHT, B_DEV)

    def term(total, index):
        targets = op_map[index][sector]
        keep = (sector[:, None] == targets[None, :]).astype(jnp.float32)
        masked = left_env[index] * keep
        envs = right_env[index].reshape(N_RIGHT, B_DEV, B_DEV)
        inner = jnp.einsum("ajc,jbc->ajb", blocks, envs, precision=lax.Precision.HIGHEST).reshape(A, B)
        return total + jnp.dot(masked, inner, precision=lax.Precision.HIGHEST, preferred_element_type=jnp.float32), None

    total, unused = lax.scan(term, jnp.zeros((A, B), jnp.float32), jnp.arange(W, dtype=jnp.int32))
    return total
```

```python
import functools

import jax
import jax.numpy as jnp
from jax import lax
from jax.experimental import pallas as pl
from jax.experimental.pallas import tpu as pltpu
from jax.sharding import PartitionSpec as P


BF16, F32 = jnp.bfloat16, jnp.float32
NT = (((1,), (1,)), ((), ()))
NN = (((1,), (0,)), ((), ()))


def halves(x):
    high = x.astype(BF16)
    return high, (x - high.astype(F32)).astype(BF16)


def product(stacked, high, low, dims):
    rows = stacked.shape[0] // 2
    both = lax.dot_general(stacked, high, dims, preferred_element_type=F32)
    cross = lax.dot_general(stacked[:rows], low, dims, preferred_element_type=F32)
    return both[:rows] + (both[rows:] + cross)


def inner_kernel(offsets, split, *refs):
    count = len(offsets)
    chunks, refs = refs[:count], refs[count:]
    if split:
        env_ref, hi_out, lo_out, env_hi, env_lo = refs[:5]
        stacked, stage_hi, stage_lo, sems = refs[5:]
    else:
        env_hi, env_lo, _, _, hi_out, lo_out = refs[:6]
        stacked, stage_hi, stage_lo, sems = refs[6:]
    rows = chunks[0].shape[0]
    term, block = pl.program_id(0), pl.program_id(1)
    steps = pl.num_programs(0) * pl.num_programs(1)
    step = term * pl.num_programs(1) + block
    width = stage_hi.shape[2]
    total = count * rows

    @pl.when(step == 0)
    def _():
        for i, chunk in enumerate(chunks):
            high, low = halves(chunk[...])
            stacked[i * rows : (i + 1) * rows] = high
            stacked[total + i * rows : total + (i + 1) * rows] = low

    if split:
        high, low = halves(env_ref[0])
        env_hi[0] = high
        env_lo[0] = low
    else:
        high, low = env_hi[0], env_lo[0]
    res_hi, res_lo = halves(product(stacked[...], high, low, NT))

    def copies(at, term, block):
        me = lax.axis_index("op")
        out = []
        for i, offset in enumerate(offsets):
            place = pl.ds(pl.multiple_of((me ^ offset) * rows, rows), rows)
            for j, (stage, dest) in enumerate(((stage_hi, hi_out), (stage_lo, lo_out))):
                out.append(
                    pltpu.make_async_copy(
                        stage.at[at, pl.ds(i * rows, rows)],
                        dest.at[term, place, pl.ds(pl.multiple_of(block * width, width), width)],
                        sems.at[at, i, j],
                    )
                )
        return out

    at = lax.rem(step, 2)

    @pl.when(step >= 2)
    def _():
        for copy in copies(at, term, block):
            copy.wait()

    stage_hi[at] = res_hi
    stage_lo[at] = res_lo
    for copy in copies(at, term, block):
        copy.start()

    @pl.when(step == steps - 1)
    def _():
        for copy in copies(1 - at, term, block) + copies(at, term, block):
            copy.wait()


def inner_call(offsets, chunks, env, inner=None, states=None, width=256):
    split = inner is None
    terms, out_rows, depth = env[0].shape
    rows = chunks[0].shape[0]
    count = len(chunks)
    env_spec = pl.BlockSpec((1, width, depth), lambda w, b: (w, b, 0))
    any_spec = pl.BlockSpec(memory_space=pl.ANY)
    env_shape = jax.ShapeDtypeStruct(env[0].shape, BF16)
    inner_shape = jax.ShapeDtypeStruct((terms, states, out_rows), BF16)
    outs = [inner_shape] * 2 + ([env_shape] * 2 if split else [])
    return pl.pallas_call(
        functools.partial(inner_kernel, offsets, split),
        grid=(terms, out_rows // width),
        in_specs=[pl.BlockSpec((rows, depth), lambda w, b: (0, 0))] * count
        + ([env_spec] if split else [env_spec] * 2 + [any_spec] * 2),
        out_specs=[any_spec] * 2 + ([env_spec] * 2 if split else []),
        out_shape=outs,
        scratch_shapes=[
            pltpu.VMEM((2 * count * rows, depth), BF16),
            pltpu.VMEM((2, count * rows, width), BF16),
            pltpu.VMEM((2, count * rows, width), BF16),
            pltpu.SemaphoreType.DMA((2, count, 2)),
        ],
        input_output_aliases={} if split else {count + 2: 0, count + 3: 1},
        cost_estimate=pl.CostEstimate(
            flops=6 * terms * count * rows * depth * out_rows,
            bytes_accessed=4 * terms * depth * out_rows * (2 if split else 1),
            transcendentals=0,
        ),
        name="inner" + "_".join(str(o) for o in offsets),
    )(*chunks, *env, *(() if split else inner))


def outer_kernel(dest, pieces, lengths, op_map, *refs):
    left = refs[:pieces]
    inner_hi, inner_lo, out, rows_in, stacked, sem = refs[pieces:]
    rows = out.shape[0]
    terms, _, states = rows_in.shape
    count = lengths.shape[0]
    me, mine = lax.axis_index("op"), lax.axis_index("right")
    target = me ^ dest

    @pl.when(pl.program_id(0) == 0)
    def _():
        per = left[0].shape[1] // rows
        slot = (target // per) ^ mine
        place = pl.ds(pl.multiple_of(lax.rem(target, per) * rows, rows), rows)
        for t in range(pieces):

            @pl.when(slot == t)
            def _():
                copy = pltpu.make_async_copy(left[t].at[:, place], rows_in, sem)
                copy.start()
                copy.wait()

        row = lax.broadcasted_iota(jnp.int32, (rows, states), 0) + target * rows
        col = lax.broadcasted_iota(jnp.int32, (rows, states), 1)
        row_sector = jnp.zeros((rows, states), jnp.int32)
        col_sector = jnp.zeros((rows, states), jnp.int32)
        end = jnp.int32(0)
        for s in range(count):
            end = end + lengths[s]
            row_sector += (row >= end).astype(jnp.int32)
            col_sector += (col >= end).astype(jnp.int32)
        for w in range(terms):
            aim = jnp.full((rows, states), -1, jnp.int32)
            for s in range(count):
                aim = jnp.where(col_sector == s, op_map[me * terms + w, s], aim)
            high, low = halves(jnp.where(row_sector == aim, rows_in[w], 0.0))
            stacked[w, :rows] = high
            stacked[w, rows:] = low

    total = product(stacked[0], inner_hi[0], inner_lo[0], NN)
    for w in range(1, terms):
        total += product(stacked[w], inner_hi[w], inner_lo[w], NN)
    out[...] = total


def outer_call(dest, rows, left, inner, lengths, op_map, width=256):
    terms, states, out_rows = inner[0].shape
    pieces = len(left)
    inner_spec = pl.BlockSpec((terms, states, width), lambda b: (0, 0, b))
    smem = pl.BlockSpec(memory_space=pltpu.SMEM)
    return pl.pallas_call(
        functools.partial(outer_kernel, dest, pieces),
        grid=(out_rows // width,),
        in_specs=[smem] * 2 + [pl.BlockSpec(memory_space=pl.ANY)] * pieces + [inner_spec] * 2,
        out_specs=pl.BlockSpec((rows, width), lambda b: (0, b)),
        out_shape=jax.ShapeDtypeStruct((rows, out_rows), F32),
        scratch_shapes=[
            pltpu.VMEM((terms, rows, states), F32),
            pltpu.VMEM((terms, 2 * rows, states), BF16),
            pltpu.SemaphoreType.DMA,
        ],
        cost_estimate=pl.CostEstimate(
            flops=6 * terms * rows * states * out_rows,
            bytes_accessed=4 * terms * states * out_rows,
            transcendentals=0,
        ),
        name=f"outer{dest}",
    )(lengths, op_map, *left, *inner)


def on_device(n_op, n_right, psi, left_env, right_env, sector_lengths, op_map):
    rows = psi.shape[0]
    states = rows * n_op
    lines = n_op // 2

    def swap(x, offset, only=None):
        pairs = [(o, o ^ offset) for o in range(n_op) if only is None or only(o // 2)]
        with jax.named_scope(f"hop{offset}"):
            return lax.ppermute(x, "op", pairs)

    def side(x, offset):
        with jax.named_scope(f"side{offset}"):
            return lax.ppermute(x, "right", [(r, r ^ offset) for r in range(n_right)])

    got = {0: psi}
    got[1] = swap(psi, 1)
    for k in range(1, lines, 2):
        got[2 * k] = swap(psi, 2 * k)
    left = {0: left_env}
    bit = n_right // 2
    while bit:
        for t in list(left):
            left[t ^ bit] = side(left[t], bit)
        bit //= 2
    for k in range(1, lines, 2):
        got[2 * k + 1] = swap(got[2 * k], 1)
    for k in range(3, lines, 2):
        got[2 * (k - 1)] = swap(got[2 * k], 2)
        got[2 * (k - 1) + 1] = swap(got[2 * (k - 1)], 1)

    *inner, env_hi, env_lo = inner_call((0,), [got[0]], [right_env], states=states)
    env = [env_hi, env_lo]
    order = [(1, 2)]
    for k in range(3, lines, 2):
        order += [(2 * k - 3, 2 * k), (2 * k + 1, 2 * k - 2)]
    order += [(2 * lines - 3,)] if lines > 2 else [(3,)]
    for offsets in order:
        inner = inner_call(offsets, [got[o] for o in offsets], env, inner, states)

    left = [left[t] for t in range(n_right)]
    part = functools.partial(
        outer_call, rows=rows, left=left, inner=inner, lengths=sector_lengths, op_map=op_map
    )
    across = {}
    for k in list(range(lines - 2, 1, -2)) + list(range(lines - 1, 0, -2)) + [0]:
        across[k] = swap(part(2 * k + 1), 1)
    sums = {}
    for k in range(lines - 2, 1, -2):
        sums[k] = part(2 * k) + across[k]
    for k in range(lines - 1, 0, -2):
        sums[k] = part(2 * k) + across[k]
        if k > 1:
            sums[k] += swap(sums[k - 1], 2)
    total = part(0) + across[0]
    for k in range(1, lines, 2):
        total += swap(sums[k], 2 * k)
    return total


def solution(mesh):
    n_op, n_right = mesh.shape["op"], mesh.shape["right"]
    in_specs = (P("op", "right"), P("op", "right", None), P("op", "right", None), P(), P())
    return jax.shard_map(
        functools.partial(on_device, n_op, n_right),
        mesh=mesh,
        in_specs=in_specs,
        out_specs=P("op", "right"),
        check_vma=False,
    )
```
